512 devices in a mesh: state: 16 (over x, y_lo, core), snap: 32 (over y_hi, z).
Axes of the slice: x: 4, y: 4 (y_hi: 2, y_lo: 2; y = y_hi * 2 + y_lo), z: 16, core: 2. Of those that a mesh axis runs over, the one named last changes fastest.
Arguments:
- direct: float32 [8192, 4096], P('state', 'snap'), may hold values from -6 to 6
- adjoint: float32 [8192, 4096], P('state', 'snap'), may hold values from -6 to 6
- cell_weight: float32 [8192], P('state'), may hold values from 0.003314563 to 0.03314563
- right_vecs: float32 [4096, 256], P('snap'), may hold values from -0.09375 to 0.09375
- left_vecs: float32 [4096, 256], P('snap'), may hold values from -0.09375 to 0.09375
- inv_root: float32 [256], replicated, may hold values from 0.5 to 2
Outputs:
- gram: float32 [4096, 4096], P('state', 'snap')
- bal_modes: float32 [8192, 256], P(('state', 'snap'))
- adj_modes: float32 [8192, 256], P(('state', 'snap'))
The draws below stay inside these ranges and needn't reach their ends.
All inputs are finite; a program needn't handle non-finite values.
Results may differ from the reference program's by a relative error of at most 0.00013.
Values sent between devices are 32-bit elements; how exact they have to be, the bound alone decides.
No kernel may reach another device: no remote copies, remote signals or barrier semaphores. Data moves between devices by JAX's collectives and lax.ppermute only.
A program may use at most 64 MiB of HBM per device.

```python
import math
import jax
import jax.numpy as jnp
from jax import lax

R = 256
NSTATE = 8192
MSNAP = 4096


def spiked(drawn, rng, source, target, shards_of, factor):
    def block_of(axis_at):
        return (jnp.arange(drawn.shape[axis_at]) // (drawn.shape[axis_at] // shards_of)).reshape((-1,) + (1,) * (drawn.ndim - 1 - axis_at))

    one_side = jax.random.permutation(rng, shards_of)[block_of(target)]
    second = (block_of(target) + shards_of // 2) % shards_of
    return jnp.where((block_of(source) == one_side) | (block_of(source) == second), factor * drawn, drawn)


def steps_of(key, extent, split, low, high):
    def one(axis_at, shards_of):
        steps = jax.random.uniform(jax.random.fold_in(jax.random.fold_in(key, 6), axis_at), (shards_of,), jnp.float32, low / len(split), high / len(split))
        return jnp.repeat(jnp.exp(steps), extent[axis_at] // shards_of).reshape((-1,) + (1,) * (len(extent) - axis_at - 1))

    factor_of = one(*split[0])
    for cut in split[1:]:
        factor_of = factor_of * one(*cut)
    return factor_of


def bell_draw(own_key, shape, spread, most, split=(), held_as=jnp.bfloat16):
    result = spread * jax.random.normal(own_key, shape, jnp.float32)
    if split:
        result = result * steps_of(own_key, shape, split, -0.22, 0.18)
    return jnp.clip(result, -most, most).astype(held_as)


def heavy_noise(rng, dims, spread, limit, pieces, heavy, kind=jnp.bfloat16):
    drawn = spread * jax.random.normal(rng, dims, jnp.float32)
    if pieces:
        drawn = drawn * steps_of(rng, dims, pieces, -0.22, 0.18)
    return jnp.clip(spiked(drawn, jax.random.fold_in(rng, 3), *heavy), -limit, limit).astype(kind)


def setup_inputs(seed: int = 0) -> dict:
    key_of = jax.random.split(jax.random.key(seed), 7)
    return {
        "direct": bell_draw(key_of[0], (NSTATE, MSNAP), 1.0, 6.0, ((0, 16), (1, 32)), jnp.float32),
        "adjoint": heavy_noise(key_of[1], (NSTATE, MSNAP), 1.0, 6.0, ((0, 16), (1, 32)), (0, 1, 32, 2.75), jnp.float32),
        "cell_weight": jnp.clip(jnp.exp(math.log(0.03314563) - 2.30258504 * jax.random.uniform(key_of[2], (NSTATE,), jnp.float32) ** steps_of(key_of[2], (NSTATE,), ((0, 16),), -0.2, 0.2)), 0.003314563, 0.03314563),
        "right_vecs": bell_draw(key_of[3], (MSNAP, R), MSNAP ** -0.5, 0.09375, ((0, 32),), jnp.float32),
        "left_vecs": bell_draw(key_of[4], (MSNAP, R), MSNAP ** -0.5, 0.09375, ((0, 32),), jnp.float32),
        "inv_root": jnp.clip(jnp.exp(jax.random.uniform(key_of[5], (R,), jnp.float32, math.log(0.5), math.log(2.0))), 0.5, 2.0),
    }


def reference(direct, adjoint, cell_weight, right_vecs, left_vecs, inv_root):
    weighted = adjoint * cell_weight[:, None]
    gram = jnp.dot(weighted.T, direct, precision=lax.Precision.HIGHEST, preferred_element_type=jnp.float32)
    bal_modes = jnp.dot(direct, right_vecs * inv_root[None, :], precision=lax.Precision.HIGHEST, preferred_element_type=jnp.float32)
    adj_modes = jnp.dot(adjoint, left_vecs * inv_root[None, :], precision=lax.Precision.HIGHEST, preferred_element_type=jnp.float32)
    return gram, bal_modes, adj_modes
```

```python
import jax
import jax.numpy as jnp
from jax import lax
from jax.sharding import Mesh, PartitionSpec as P

AXES = ("x", "l", "c", "h", "z")
SIZES = (4, 2, 2, 2, 16)
PREC = lax.Precision.HIGH


def _swap_pairs():
    pairs = []
    for x in range(4):
        for h in range(2):
            high, low = divmod(x, 2)
            pairs.append((x * 2 + h, (h * 2 + low) * 2 + high))
    return pairs


def _dot(a, b):
    return jnp.dot(a, b, precision=PREC, preferred_element_type=jnp.float32)


def local(direct, adjoint, cell_weight, right_vecs, left_vecs, inv_root):
    h = lax.axis_index("h")
    cells, cols = direct.shape
    modes = right_vecs.shape[1]
    half = cells // 2

    gathered = lax.all_gather(adjoint, "z", axis=0, tiled=False)

    mine = lax.dynamic_slice_in_dim(adjoint, h * half, half, 0)
    theirs = lax.dynamic_slice_in_dim(adjoint, (1 - h) * half, half, 0)
    sent = jnp.concatenate(
        [direct, theirs, right_vecs[:, :cols], right_vecs[:, cols:], left_vecs[:, :cols], left_vecs[:, cols:]], axis=0
    )
    got = lax.ppermute(sent, "h", [(0, 1), (1, 0)])
    other_direct = got[:cells]
    other_adjoint = got[cells : cells + half]
    rest = got[cells + half :].reshape(2, 2, cols, cols)
    other_right = jnp.concatenate([rest[0, 0], rest[0, 1]], axis=1)
    other_left = jnp.concatenate([rest[1, 0], rest[1, 1]], axis=1)

    own_rows = lax.dynamic_slice_in_dim(direct, h * half, half, 0)
    other_rows = lax.dynamic_slice_in_dim(other_direct, h * half, half, 0)
    scale = inv_root[None, :]
    bal = _dot(
        jnp.concatenate([own_rows, other_rows], axis=1),
        jnp.concatenate([right_vecs, other_right], axis=0) * scale,
    )
    adj = _dot(
        jnp.concatenate([mine, other_adjoint], axis=1),
        jnp.concatenate([left_vecs, other_left], axis=0) * scale,
    )
    terms = jnp.concatenate([bal, adj], axis=1).reshape(16, half // 16, 2 * modes)
    summed = lax.all_to_all(terms, "z", 0, 0, tiled=False).sum(0)

    weight = cell_weight[:, None]
    both = jnp.where(
        h == 0,
        jnp.concatenate([direct, other_direct], axis=1),
        jnp.concatenate([other_direct, direct], axis=1),
    ) * weight
    gathered, both, summed = lax.optimization_barrier((gathered, both, summed))

    product = lax.dot_general(
        gathered, both, (((1,), (0,)), ((), ())), precision=PREC, preferred_element_type=jnp.float32
    )
    product = jnp.stack([product[:, :, :cols], product[:, :, cols:]]).reshape(2, 2, 2, 2, 2, cols, cols)
    product = product.transpose(3, 0, 1, 2, 4, 5, 6).reshape(2, 8 * 2 * cols, cols)
    product = lax.all_to_all(product, "c", 0, 0, tiled=False).sum(0)
    product = lax.all_to_all(product.reshape(8, 2 * cols, cols), ("x", "l"), 0, 0, tiled=False).sum(0)
    gram = lax.ppermute(product, ("x", "h"), _swap_pairs())
    return (gram, summed[:, :modes], summed[:, modes:])


def solution(mesh):
    fine = Mesh(mesh.devices.reshape(SIZES), AXES)
    state, snap = ("x", "l", "c"), ("h", "z")
    in_specs = (P(state, snap), P(state, snap), P(state), P(snap, None), P(snap, None), P())
    out_specs = (P(state, snap), P(state + snap, None), P(state + snap, None))
    return jax.shard_map(local, mesh=fine, in_specs=in_specs, out_specs=out_specs, check_vma=False)
```

```python
import jax
import jax.numpy as jnp
from jax import lax
from jax.sharding import Mesh, PartitionSpec as P

AXES = ("x", "l", "c", "h", "z")
SIZES = (4, 2, 2, 2, 16)
PREC = lax.Precision.HIGH


def _ring_pairs(steps_up, steps_down):
    pairs = []
    for z in range(16):
        if steps_up:
            pairs.append((z, (z + 1) % 16))
        if steps_down:
            pairs.append((16 + z, 16 + (z - 1) % 16))
    return pairs


def _block_of(i, c, z):
    return (z - i if c == 0 else z + 1 + i) % 16


def _home_pairs(turn):
    pairs = []
    for x in range(4):
        for l in range(2):
            for c in range(2):
                for h in range(2):
                    for z in range(16):
                        block = _block_of(x * 2 + l, c, z)
                        state = h * 8 + block // 2
                        pairs.append(((((x * 2 + l) * 2 + c) * 2 + h) * 16 + z, (state * 2 + (block % 2 ^ turn)) * 16 + z))
    return pairs


def _dot(a, b):
    return jnp.dot(a, b, precision=PREC, preferred_element_type=jnp.float32)


def _cross(a, b):
    return lax.dot_general(a, b, (((0,), (0,)), ((), ())), precision=PREC, preferred_element_type=jnp.float32)


def local(direct, adjoint, cell_weight, right_vecs, left_vecs, inv_root):
    h, z, c = lax.axis_index("h"), lax.axis_index("z"), lax.axis_index("c")
    index = lax.axis_index("x") * 2 + lax.axis_index("l")
    cells, cols = direct.shape
    modes = right_vecs.shape[1]
    swap = [(0, 1), (1, 0)]

    other_adjoint = lax.ppermute(adjoint, "c", swap)
    other_direct = lax.ppermute(direct, "h", swap)

    scale = inv_root[None, :]
    terms = jnp.concatenate([_dot(direct, right_vecs * scale), _dot(adjoint, left_vecs * scale)], axis=1)
    terms = terms.reshape(2, 16, cells // 32, 2 * modes).transpose(1, 0, 2, 3).reshape(cells, 2 * modes)
    part = lax.psum_scatter(terms, "z", scatter_dimension=0, tiled=True).reshape(2, cells // 32, 2 * modes)

    both = jnp.where(
        h == 0,
        jnp.concatenate([direct, other_direct], axis=1),
        jnp.concatenate([other_direct, direct], axis=1),
    ) * cell_weight[:, None]
    other_both = lax.ppermute(both, "c", swap)

    own, other = adjoint, other_adjoint
    blocks = []
    for step in range(9):
        if step < 8:
            blocks.append((own, other))
        if step == 8:
            last = (own, other)
        if step < 8:
            pairs = _ring_pairs(step < 7, True)
            own = lax.ppermute(own, ("c", "z"), pairs)
            other = lax.ppermute(other, ("c", "z"), pairs)
    blocks.append(last)
    products = [_cross(a, both) + _cross(b, other_both) for a, b in blocks]
    product = jnp.stack([jnp.where(c == 0, products[i], products[i + 1]) for i in range(8)])
    product = lax.all_to_all(product, ("x", "l"), 0, 0, tiled=False).sum(0)

    odd = (jnp.where(c == 0, z + index, z + 1 + index) % 2) == 1
    first, second = product[:, :cols], product[:, cols:]
    home0 = lax.ppermute(jnp.where(odd, second, first), AXES, _home_pairs(0))
    home1 = lax.ppermute(jnp.where(odd, first, second), AXES, _home_pairs(1))
    gram = jnp.where(h == 0, jnp.concatenate([home0, home1]), jnp.concatenate([home1, home0]))

    keep = lax.dynamic_index_in_dim(part, h, 0, keepdims=False)
    away = lax.dynamic_index_in_dim(part, 1 - h, 0, keepdims=False)
    summed = keep + lax.ppermute(away, "h", swap)
    return (gram, summed[:, :modes], summed[:, modes:])


def solution(mesh):
    fine = Mesh(mesh.devices.reshape(SIZES), AXES)
    state, snap = ("x", "l", "c"), ("h", "z")
    in_specs = (P(state, snap), P(state, snap), P(state), P(snap, None), P(snap, None), P())
    out_specs = (P(state, snap), P(state + snap, None), P(state + snap, None))
    return jax.shard_map(local, mesh=fine, in_specs=in_specs, out_specs=out_specs, check_vma=False)
```

```python
import jax
import jax.numpy as jnp
from jax import lax
from jax.sharding import Mesh, PartitionSpec as P


AXES = ("x", "l", "c", "h", "g", "q")
SIZES = (4, 2, 2, 2, 8, 2)
PREC = lax.Precision.HIGH
SWAP = [(0, 1), (1, 0)]


def _ring_pairs(up):
    pairs = []
    for g in range(8):
        if up:
            pairs.append((g, (g + 1) % 8))
        pairs.append((8 + g, 8 + (g - 1) % 8))
    return pairs


def _home_pairs():
    pairs = []
    for x in range(4):
        for l in range(2):
            for c in range(2):
                for h in range(2):
                    for g in range(8):
                        low = (g - x if c == 0 else g + 1 + x) % 8
                        here = (((x * 2 + l) * 2 + c) * 2 + h) * 8 + g
                        pairs.append((here, ((h * 8 + low) * 2 + l) * 8 + g))
    return pairs


def _dot(a, b):
    return jnp.dot(a, b, precision=PREC, preferred_element_type=jnp.float32)


def _cross(a, b):
    return lax.dot_general(a, b, (((0,), (0,)), ((), ())), precision=PREC, preferred_element_type=jnp.float32)


def _beside(index, mine, theirs):
    return jnp.where(
        index == 0, jnp.concatenate([mine, theirs], axis=1), jnp.concatenate([theirs, mine], axis=1)
    )


def local(direct, adjoint, cell_weight, right_vecs, left_vecs, inv_root):
    c, h, q = lax.axis_index("c"), lax.axis_index("h"), lax.axis_index("q")
    cells, cols = direct.shape
    modes = right_vecs.shape[1]

    other = lax.ppermute(adjoint, "c", SWAP)
    next_own = lax.ppermute(adjoint, ("c", "g"), _ring_pairs(False))
    next_other = lax.ppermute(other, ("c", "g"), _ring_pairs(False))
    own = jnp.where(c == 0, adjoint, next_own)
    other = jnp.where(c == 0, other, next_other)

    scale = inv_root[None, :]
    terms = jnp.concatenate([_dot(direct, right_vecs * scale), _dot(adjoint, left_vecs * scale)], axis=1)
    terms = terms.reshape(2, 16, cells // 32, 2 * modes).transpose(1, 0, 2, 3).reshape(cells, 2 * modes)
    own, other, terms = lax.optimization_barrier((own, other, terms))
    part = lax.psum_scatter(terms, ("g", "q"), scatter_dimension=0, tiled=True).reshape(2, cells // 32, 2 * modes)

    pair = _beside(q, direct, lax.ppermute(direct, "q", SWAP)) * cell_weight[:, None]
    both = _beside(h, pair, lax.ppermute(pair, "h", SWAP))
    other_both = lax.ppermute(both, "c", SWAP)

    pieces = []
    for step in range(4):
        product = _cross(own, both) + _cross(other, other_both)
        piece = jnp.stack([product[:, k * cols : (k + 1) * cols] for k in range(4)])
        if step < 3:
            own = lax.ppermute(own, ("c", "g"), _ring_pairs(True))
            other = lax.ppermute(other, ("c", "g"), _ring_pairs(True))
        pieces.append(lax.optimization_barrier(piece))

    got = lax.all_to_all(jnp.concatenate(pieces), ("x", "l", "q"), 0, 0, tiled=True)
    block = got.reshape(8, 2 * cols, cols).sum(0)
    gram = lax.ppermute(block, ("x", "l", "c", "h", "g"), _home_pairs())

    keep = lax.dynamic_index_in_dim(part, h, 0, keepdims=False)
    away = lax.dynamic_index_in_dim(part, 1 - h, 0, keepdims=False)
    summed = keep + lax.ppermute(away, "h", SWAP)
    return (gram, summed[:, :modes], summed[:, modes:])


def solution(mesh):
    fine = Mesh(mesh.devices.reshape(SIZES), AXES)
    state, snap = ("x", "l", "c"), ("h", "g", "q")
    in_specs = (P(state, snap), P(state, snap), P(state), P(snap, None), P(snap, None), P())
    out_specs = (P(state, snap), P(state + snap, None), P(state + snap, None))


    return jax.shard_map(local, mesh=fine, in_specs=in_specs, out_specs=out_specs, check_vma=False)
```

```python
import jax
import jax.numpy as jnp
from jax import lax
from jax.sharding import Mesh, PartitionSpec as P


AXES = ("x", "l", "c", "h", "g", "q")
SIZES = (4, 2, 2, 2, 8, 2)
PREC = lax.Precision.HIGH
SWAP = [(0, 1), (1, 0)]


def _ring_pairs(up):
    pairs = []
    for g in range(8):
        if up:
            pairs.append((g, (g + 1) % 8))
        pairs.append((8 + g, 8 + (g - 1) % 8))
    return pairs


def _home_pairs(turn):
    pairs = []
    for here in range(512):
        rest, q = divmod(here, 2)
        rest, g = divmod(rest, 8)
        rest, h = divmod(rest, 2)
        rest, c = divmod(rest, 2)
        x, l = divmod(rest, 2)
        arrival = 2 * (turn ^ q) + x // 2
        low = (g - arrival if c == 0 else g + 1 + arrival) % 8
        pairs.append((here, (((h * 8 + low) * 2 + x % 2) * 8 + g) * 2 + l))
    return pairs


def _dot(a, b):
    return jnp.dot(a, b, precision=PREC, preferred_element_type=jnp.float32)


def _cross(a, b):
    return lax.dot_general(a, b, (((0,), (0,)), ((), ())), precision=PREC, preferred_element_type=jnp.float32)


def _beside(index, mine, theirs):
    return jnp.where(
        index == 0, jnp.concatenate([mine, theirs], axis=1), jnp.concatenate([theirs, mine], axis=1)
    )


def local(direct, adjoint, cell_weight, right_vecs, left_vecs, inv_root):
    c, h, q = lax.axis_index("c"), lax.axis_index("h"), lax.axis_index("q")
    cells, cols = direct.shape
    modes = right_vecs.shape[1]

    next_direct = lax.ppermute(direct, "q", SWAP)
    next_own = lax.ppermute(adjoint, ("c", "g"), _ring_pairs(False))
    other = lax.ppermute(adjoint, "c", SWAP)
    next_other = lax.ppermute(other, ("c", "g"), _ring_pairs(False))
    own = jnp.where(c == 0, adjoint, next_own)
    other = jnp.where(c == 0, other, next_other)

    scale = inv_root[None, :]
    terms = jnp.concatenate([_dot(direct, right_vecs * scale), _dot(adjoint, left_vecs * scale)], axis=1)
    half = cells // 2
    keep = lax.dynamic_slice_in_dim(terms, h * half, half, 0)
    away = lax.dynamic_slice_in_dim(terms, (1 - h) * half, half, 0)
    summed = lax.psum_scatter(keep + lax.ppermute(away, "h", SWAP), ("g", "q"), scatter_dimension=0, tiled=True)

    pair = _beside(q, direct, next_direct) * cell_weight[:, None]
    both = _beside(h, pair, lax.ppermute(pair, "h", SWAP))
    other_both = lax.ppermute(both, "c", SWAP)

    pieces = []
    for step in range(4):
        product = _cross(own, both) + _cross(other, other_both)
        piece = jnp.stack([product[:, k * cols : (k + 1) * cols] for k in range(4)])
        if step < 3:
            own = lax.ppermute(own, ("c", "g"), _ring_pairs(True))
            other = lax.ppermute(other, ("c", "g"), _ring_pairs(True))
        pieces.append(lax.optimization_barrier(piece))

    sums = []
    for chunk in range(2):
        chunk_pieces = jnp.concatenate(pieces[2 * chunk : 2 * chunk + 2])
        sums.append(lax.all_to_all(chunk_pieces, ("x", "l"), 0, 0, tiled=True).sum(0))
    home0 = lax.ppermute(jnp.where(q == 0, sums[0], sums[1]), AXES, _home_pairs(0))
    home1 = lax.ppermute(jnp.where(q == 0, sums[1], sums[0]), AXES, _home_pairs(1))

    low = (lax.axis_index("x") % 2) * 4 + lax.axis_index("l") * 2 + c
    behind = (lax.axis_index("g") - low) % 8
    arrival = jnp.where(behind < 4, behind, 7 - behind)
    gram = jnp.where(arrival < 2, jnp.concatenate([home0, home1]), jnp.concatenate([home1, home0]))
    return (gram, summed[:, :modes], summed[:, modes:])


def solution(mesh):
    fine = Mesh(mesh.devices.reshape(SIZES), AXES)
    state, snap = ("x", "l", "c"), ("h", "g", "q")
    in_specs = (P(state, snap), P(state, snap), P(state), P(snap, None), P(snap, None), P())
    out_specs = (P(state, snap), P(state + snap, None), P(state + snap, None))


    return jax.shard_map(local, mesh=fine, in_specs=in_specs, out_specs=out_specs, check_vma=False)
```

```python
import jax
import jax.numpy as jnp
from jax import lax
from jax.sharding import Mesh, PartitionSpec as P


AXES = ("x", "l", "c", "h", "g", "q")
SIZES = (4, 2, 2, 2, 8, 2)
PREC = lax.Precision.HIGH
SWAP = [(0, 1), (1, 0)]


def _ring_pairs(up):
    pairs = []
    for g in range(8):
        if up:
            pairs.append((g, (g + 1) % 8))
        pairs.append((8 + g, 8 + (g - 1) % 8))
    return pairs


def _home_pairs(turn):
    pairs = []
    for here in range(512):
        rest, q = divmod(here, 2)
        rest, g = divmod(rest, 8)
        rest, h = divmod(rest, 2)
        rest, c = divmod(rest, 2)
        x, l = divmod(rest, 2)
        arrival = 2 * (turn ^ q) + x // 2
        low = (g - arrival if c == 0 else g + 1 + arrival) % 8
        pairs.append((here, (((h * 8 + low) * 2 + x % 2) * 8 + g) * 2 + l))
    return pairs


def _dot(a, b):
    return jnp.dot(a, b, precision=PREC, preferred_element_type=jnp.float32)


def _cross(a, b):
    return lax.dot_general(a, b, (((0,), (0,)), ((), ())), precision=PREC, preferred_element_type=jnp.float32)


def _beside(index, mine, theirs):
    return jnp.where(
        index == 0, jnp.concatenate([mine, theirs], axis=1), jnp.concatenate([theirs, mine], axis=1)
    )


def local(direct, adjoint, cell_weight, right_vecs, left_vecs, inv_root):
    c, h, q = lax.axis_index("c"), lax.axis_index("h"), lax.axis_index("q")
    cells, cols = direct.shape
    modes = right_vecs.shape[1]

    scale = inv_root[None, :]
    terms = jnp.concatenate([_dot(direct, right_vecs * scale), _dot(adjoint, left_vecs * scale)], axis=1)
    half = cells // 2
    away = lax.ppermute(lax.dynamic_slice_in_dim(terms, (1 - h) * half, half, 0), "h", SWAP)
    next_direct = lax.ppermute(direct, "q", SWAP)
    next_own = lax.ppermute(adjoint, ("c", "g"), _ring_pairs(False))
    other = lax.ppermute(adjoint, "c", SWAP)
    next_other = lax.ppermute(other, ("c", "g"), _ring_pairs(False))
    own = jnp.where(c == 0, adjoint, next_own)
    other = jnp.where(c == 0, other, next_other)

    terms = away + lax.dynamic_slice_in_dim(terms, h * half, half, 0)
    summed = lax.psum_scatter(terms, ("g", "q"), scatter_dimension=0, tiled=True)

    pair = _beside(q, direct, next_direct) * cell_weight[:, None]
    both = _beside(h, pair, lax.ppermute(pair, "h", SWAP))
    other_both = lax.ppermute(both, "c", SWAP)

    pieces = []
    for step in range(4):
        product = _cross(own, both) + _cross(other, other_both)
        piece = jnp.stack([product[:, k * cols : (k + 1) * cols] for k in range(4)])
        if step < 3:
            own = lax.ppermute(own, ("c", "g"), _ring_pairs(True))
            other = lax.ppermute(other, ("c", "g"), _ring_pairs(True))
        pieces.append(lax.optimization_barrier(piece))
        if step == 2:
            early = lax.all_to_all(jnp.concatenate(pieces[:2]), ("x", "l"), 0, 0, tiled=True).sum(0)
            own, other, pieces, early = lax.optimization_barrier((own, other, pieces, early))

    late = lax.all_to_all(jnp.concatenate(pieces[2:]), ("x", "l"), 0, 0, tiled=True).sum(0)
    home0 = lax.ppermute(jnp.where(q == 0, early, late), AXES, _home_pairs(0))
    home1 = lax.ppermute(jnp.where(q == 0, late, early), AXES, _home_pairs(1))

    low = (lax.axis_index("x") % 2) * 4 + lax.axis_index("l") * 2 + c
    behind = (lax.axis_index("g") - low) % 8
    arrival = jnp.where(behind < 4, behind, 7 - behind)
    gram = jnp.where(arrival < 2, jnp.concatenate([home0, home1]), jnp.concatenate([home1, home0]))
    return (gram, summed[:, :modes], summed[:, modes:])


def solution(mesh):
    fine = Mesh(mesh.devices.reshape(SIZES), AXES)
    state, snap = ("x", "l", "c"), ("h", "g", "q")
    in_specs = (P(state, snap), P(state, snap), P(state), P(snap, None), P(snap, None), P())
    out_specs = (P(state, snap), P(state + snap, None), P(state + snap, None))


    return jax.shard_map(local, mesh=fine, in_specs=in_specs, out_specs=out_specs, check_vma=False)
```

```python
import jax
import jax.numpy as jnp
from jax import lax
from jax.sharding import Mesh, PartitionSpec as P


AXES = ("x", "l", "c", "h", "g", "q")
SIZES = (4, 2, 2, 2, 8, 2)
PREC = lax.Precision.HIGH
SWAP = [(0, 1), (1, 0)]


def _ring_pairs(up):
    pairs = []
    for g in range(8):
        if up:
            pairs.append((g, (g + 1) % 8))
        pairs.append((8 + g, 8 + (g - 1) % 8))
    return pairs


def _home_pairs(turn):
    pairs = []
    for here in range(512):
        rest, q = divmod(here, 2)
        rest, g = divmod(rest, 8)
        rest, h = divmod(rest, 2)
        rest, c = divmod(rest, 2)
        x, l = divmod(rest, 2)
        arrival = 2 * (turn ^ q) + x // 2
        low = (g - arrival if c == 0 else g + 1 + arrival) % 8
        pairs.append((here, (((h * 8 + low) * 2 + x % 2) * 8 + g) * 2 + l))
    return pairs


def _dot(a, b):
    return jnp.dot(a, b, precision=PREC, preferred_element_type=jnp.float32)


def _cross(a, b):
    return lax.dot_general(a, b, (((0,), (0,)), ((), ())), precision=PREC, preferred_element_type=jnp.float32)


def _beside(index, mine, theirs):
    return jnp.where(
        index == 0, jnp.concatenate([mine, theirs], axis=1), jnp.concatenate([theirs, mine], axis=1)
    )


def local(direct, adjoint, cell_weight, right_vecs, left_vecs, inv_root):
    c, h, q = lax.axis_index("c"), lax.axis_index("h"), lax.axis_index("q")
    cells, cols = direct.shape
    modes = right_vecs.shape[1]

    next_direct = lax.ppermute(direct, "q", SWAP)
    next_own = lax.ppermute(adjoint, ("c", "g"), _ring_pairs(False))
    other = lax.ppermute(adjoint, "c", SWAP)
    other, direct_after, adjoint_after = lax.optimization_barrier((other, direct, adjoint))
    next_other = lax.ppermute(other, ("c", "g"), _ring_pairs(False))
    own = jnp.where(c == 0, adjoint, next_own)
    other = jnp.where(c == 0, other, next_other)

    scale = inv_root[None, :]
    terms = jnp.concatenate(
        [_dot(direct_after, right_vecs * scale), _dot(adjoint_after, left_vecs * scale)], axis=1
    )
    half = cells // 2
    away = lax.ppermute(lax.dynamic_slice_in_dim(terms, (1 - h) * half, half, 0), "h", SWAP)
    terms = away + lax.dynamic_slice_in_dim(terms, h * half, half, 0)
    summed = lax.psum_scatter(terms, ("g", "q"), scatter_dimension=0, tiled=True)

    pair = _beside(q, direct, next_direct) * cell_weight[:, None]
    both = _beside(h, pair, lax.ppermute(pair, "h", SWAP))
    other_both = lax.ppermute(both, "c", SWAP)

    pieces = []
    for step in range(4):
        product = _cross(own, both) + _cross(other, other_both)
        piece = jnp.stack([product[:, k * cols : (k + 1) * cols] for k in range(4)])
        if step < 3:
            own = lax.ppermute(own, ("c", "g"), _ring_pairs(True))
            other = lax.ppermute(other, ("c", "g"), _ring_pairs(True))
        pieces.append(lax.optimization_barrier(piece))
        if step == 2:
            early = lax.all_to_all(jnp.concatenate(pieces[:2]), ("x", "l"), 0, 0, tiled=True).sum(0)
            own, other, pieces, early = lax.optimization_barrier((own, other, pieces, early))

    late = lax.all_to_all(jnp.concatenate(pieces[2:]), ("x", "l"), 0, 0, tiled=True).sum(0)
    home0 = lax.ppermute(jnp.where(q == 0, early, late), AXES, _home_pairs(0))
    home1 = lax.ppermute(jnp.where(q == 0, late, early), AXES, _home_pairs(1))

    low = (lax.axis_index("x") % 2) * 4 + lax.axis_index("l") * 2 + c
    behind = (lax.axis_index("g") - low) % 8
    arrival = jnp.where(behind < 4, behind, 7 - behind)
    gram = jnp.where(arrival < 2, jnp.concatenate([home0, home1]), jnp.concatenate([home1, home0]))
    return (gram, summed[:, :modes], summed[:, modes:])


def solution(mesh):
    fine = Mesh(mesh.devices.reshape(SIZES), AXES)
    state, snap = ("x", "l", "c"), ("h", "g", "q")
    in_specs = (P(state, snap), P(state, snap), P(state), P(snap, None), P(snap, None), P())
    out_specs = (P(state, snap), P(state + snap, None), P(state + snap, None))


    return jax.shard_map(local, mesh=fine, in_specs=in_specs, out_specs=out_specs, check_vma=False)
```

```python
import jax
import jax.numpy as jnp
from jax import lax
from jax.sharding import Mesh, PartitionSpec as P


AXES = ("x", "l", "c", "h", "g", "q")
SIZES = (4, 2, 2, 2, 8, 2)
PREC = lax.Precision.HIGH
SWAP = [(0, 1), (1, 0)]


def _ring_pairs(up):
    pairs = []
    for g in range(8):
        if up:
            pairs.append((g, (g + 1) % 8))
        pairs.append((8 + g, 8 + (g - 1) % 8))
    return pairs


def _home_pairs(turn):
    pairs = []
    for here in range(512):
        rest, q = divmod(here, 2)
        rest, g = divmod(rest, 8)
        rest, h = divmod(rest, 2)
        rest, c = divmod(rest, 2)
        x, l = divmod(rest, 2)
        arrival = 2 * (turn ^ q) + x // 2
        low = (g - arrival if c == 0 else g + 1 + arrival) % 8
        pairs.append((here, (((h * 8 + low) * 2 + x % 2) * 8 + g) * 2 + l))
    return pairs


def _dot(a, b):
    return jnp.dot(a, b, precision=PREC, preferred_element_type=jnp.float32)


def _cross(a, b):
    return lax.dot_general(a, b, (((0,), (0,)), ((), ())), precision=PREC, preferred_element_type=jnp.float32)


def _beside(index, mine, theirs):
    return jnp.where(
        index == 0, jnp.concatenate([mine, theirs], axis=1), jnp.concatenate([theirs, mine], axis=1)
    )


def local(direct, adjoint, cell_weight, right_vecs, left_vecs, inv_root):
    c, h, q = lax.axis_index("c"), lax.axis_index("h"), lax.axis_index("q")
    cells, cols = direct.shape
    modes = right_vecs.shape[1]

    next_direct = lax.ppermute(direct, "q", SWAP)
    next_own = lax.ppermute(adjoint, ("c", "g"), _ring_pairs(False))
    other = lax.ppermute(adjoint, "c", SWAP)
    scale = inv_root[None, :]
    terms = jnp.concatenate([_dot(direct, right_vecs * scale), _dot(adjoint, left_vecs * scale)], axis=1)
    rows = cells // 32
    terms = terms.reshape(2, 8, 2, rows, 2 * modes).transpose(2, 1, 0, 3, 4).reshape(2, cells // 2, 2 * modes)
    away = lax.dynamic_index_in_dim(terms, 1 - q, 0, keepdims=False)
    away, other = lax.optimization_barrier((away, other))
    away = lax.ppermute(away, "q", SWAP)
    next_other = lax.ppermute(other, ("c", "g"), _ring_pairs(False))
    own = jnp.where(c == 0, adjoint, next_own)
    other = jnp.where(c == 0, other, next_other)

    terms = away + lax.dynamic_index_in_dim(terms, q, 0, keepdims=False)
    part = lax.psum_scatter(terms, "g", scatter_dimension=0, tiled=True).reshape(2, rows, 2 * modes)

    pair = _beside(q, direct, next_direct) * cell_weight[:, None]
    both = _beside(h, pair, lax.ppermute(pair, "h", SWAP))
    other_both = lax.ppermute(both, "c", SWAP)

    pieces = []
    for step in range(4):
        product = _cross(own, both) + _cross(other, other_both)
        piece = jnp.stack([product[:, k * cols : (k + 1) * cols] for k in range(4)])
        if step < 3:
            own = lax.ppermute(own, ("c", "g"), _ring_pairs(True))
            other = lax.ppermute(other, ("c", "g"), _ring_pairs(True))
        pieces.append(lax.optimization_barrier(piece))
        if step == 2:
            early = lax.all_to_all(jnp.concatenate(pieces[:2]), ("x", "l"), 0, 0, tiled=True).sum(0)
            own, other, pieces, early = lax.optimization_barrier((own, other, pieces, early))

    late = lax.all_to_all(jnp.concatenate(pieces[2:]), ("x", "l"), 0, 0, tiled=True).sum(0)
    home0 = lax.ppermute(jnp.where(q == 0, early, late), AXES, _home_pairs(0))
    home1 = lax.ppermute(jnp.where(q == 0, late, early), AXES, _home_pairs(1))

    low = (lax.axis_index("x") % 2) * 4 + lax.axis_index("l") * 2 + c
    behind = (lax.axis_index("g") - low) % 8
    arrival = jnp.where(behind < 4, behind, 7 - behind)
    gram = jnp.where(arrival < 2, jnp.concatenate([home0, home1]), jnp.concatenate([home1, home0]))

    keep = lax.dynamic_index_in_dim(part, h, 0, keepdims=False)
    away = lax.dynamic_index_in_dim(part, 1 - h, 0, keepdims=False)
    summed = keep + lax.ppermute(away, "h", SWAP)
    return (gram, summed[:, :modes], summed[:, modes:])


def solution(mesh):
    fine = Mesh(mesh.devices.reshape(SIZES), AXES)
    state, snap = ("x", "l", "c"), ("h", "g", "q")
    in_specs = (P(state, snap), P(state, snap), P(state), P(snap, None), P(snap, None), P())
    out_specs = (P(state, snap), P(state + snap, None), P(state + snap, None))


    return jax.shard_map(local, mesh=fine, in_specs=in_specs, out_specs=out_specs, check_vma=False)
```

```python
import jax
import jax.numpy as jnp
from jax import lax
from jax.sharding import Mesh, PartitionSpec as P


AXES = ("x", "l", "c", "h", "g", "q")
SIZES = (4, 2, 2, 2, 8, 2)
PREC = lax.Precision.HIGH
SWAP = [(0, 1), (1, 0)]


RING = [(g, (g + 1) % 8) for g in range(8)] + [(8 + g, 8 + (g - 1) % 8) for g in range(8)]


def _home_pairs(turn):
    pairs = []
    for here in range(512):
        rest, q = divmod(here, 2)
        rest, g = divmod(rest, 8)
        rest, h = divmod(rest, 2)
        rest, c = divmod(rest, 2)
        x, l = divmod(rest, 2)
        arrival = 2 * (turn ^ q) + x // 2
        low = (g - arrival if c == 0 else g + 1 + arrival) % 8
        pairs.append((here, (((h * 8 + low) * 2 + x % 2) * 8 + g) * 2 + l))
    return pairs


def _dot(a, b):
    return jnp.dot(a, b, precision=PREC, preferred_element_type=jnp.float32)


def _cross(a, b):
    return lax.dot_general(a, b, (((0,), (0,)), ((), ())), precision=PREC, preferred_element_type=jnp.float32)


def _beside(index, mine, theirs):
    return jnp.where(
        index == 0, jnp.concatenate([mine, theirs], axis=1), jnp.concatenate([theirs, mine], axis=1)
    )


def local(direct, adjoint, cell_weight, right_vecs, left_vecs, inv_root):
    c, h, q = lax.axis_index("c"), lax.axis_index("h"), lax.axis_index("q")
    cells, cols = direct.shape
    modes = right_vecs.shape[1]

    scale = inv_root[None, :]
    terms = jnp.concatenate([_dot(direct, right_vecs * scale), _dot(adjoint, left_vecs * scale)], axis=1)
    terms = terms.reshape(2, 16, cells // 32, 2 * modes).transpose(1, 0, 2, 3).reshape(cells, 2 * modes)
    terms, kept = lax.optimization_barrier((terms, adjoint))
    part = lax.psum_scatter(terms, ("g", "q"), scatter_dimension=0, tiled=True)
    part = part.reshape(2, cells // 32, 2 * modes)

    next_direct = lax.ppermute(direct, "q", SWAP)
    other = lax.ppermute(kept, "c", SWAP)
    pair = _beside(q, direct, next_direct) * cell_weight[:, None]
    both = _beside(h, pair, lax.ppermute(pair, "h", SWAP))
    other_both = lax.ppermute(both, "c", SWAP)

    def product(mine, theirs):
        return _cross(mine, both) + _cross(theirs, other_both)

    def pieces(below, above):
        rows = jnp.where(c == 0, below, above)
        return lax.optimization_barrier(jnp.stack([rows[:, k * cols : (k + 1) * cols] for k in range(4)]))

    own = adjoint
    products = [product(own, other)]
    for _ in range(3):
        own = lax.ppermute(own, ("c", "g"), RING)
        other = lax.ppermute(other, ("c", "g"), RING)
        products.append(product(own, other))
    own = lax.ppermute(own, ("c", "g"), RING)
    first = jnp.concatenate([pieces(products[0], products[1]), pieces(products[1], products[2])])
    early = lax.all_to_all(first, ("x", "l"), 0, 0, tiled=True).sum(0)
    own, early = lax.optimization_barrier((own, early))
    opposite = _cross(own, both)
    opposite = opposite + lax.ppermute(opposite, "c", SWAP)
    second = jnp.concatenate([pieces(products[2], products[3]), pieces(products[3], opposite)])
    late = lax.all_to_all(second, ("x", "l"), 0, 0, tiled=True).sum(0)
    home0 = lax.ppermute(jnp.where(q == 0, early, late), AXES, _home_pairs(0))
    home1 = lax.ppermute(jnp.where(q == 0, late, early), AXES, _home_pairs(1))

    low = (lax.axis_index("x") % 2) * 4 + lax.axis_index("l") * 2 + c
    behind = (lax.axis_index("g") - low) % 8
    arrival = jnp.where(behind < 4, behind, 7 - behind)
    gram = jnp.where(arrival < 2, jnp.concatenate([home0, home1]), jnp.concatenate([home1, home0]))

    keep = lax.dynamic_index_in_dim(part, h, 0, keepdims=False)
    away = lax.dynamic_index_in_dim(part, 1 - h, 0, keepdims=False)
    summed = keep + lax.ppermute(away, "h", SWAP)
    return (gram, summed[:, :modes], summed[:, modes:])


def solution(mesh):
    fine = Mesh(mesh.devices.reshape(SIZES), AXES)
    state, snap = ("x", "l", "c"), ("h", "g", "q")
    in_specs = (P(state, snap), P(state, snap), P(state), P(snap, None), P(snap, None), P())
    out_specs = (P(state, snap), P(state + snap, None), P(state + snap, None))


    return jax.shard_map(local, mesh=fine, in_specs=in_specs, out_specs=out_specs, check_vma=False)
```

```python
import jax
import jax.numpy as jnp
from jax import lax
from jax.sharding import Mesh, PartitionSpec as P


AXES = ("x", "l", "c", "h", "g", "q")
SIZES = (4, 2, 2, 2, 8, 2)
PREC = lax.Precision.HIGH
SWAP = [(0, 1), (1, 0)]


def _ring_pairs(up):
    pairs = []
    for g in range(8):
        if up:
            pairs.append((g, (g + 1) % 8))
        pairs.append((8 + g, 8 + (g - 1) % 8))
    return pairs


def _home_pairs(turn):
    pairs = []
    for here in range(512):
        rest, q = divmod(here, 2)
        rest, g = divmod(rest, 8)
        rest, h = divmod(rest, 2)
        rest, c = divmod(rest, 2)
        x, l = divmod(rest, 2)
        arrival = 2 * (turn ^ q) + x // 2
        low = (g - arrival if c == 0 else g + 1 + arrival) % 8
        pairs.append((here, (((h * 8 + low) * 2 + x % 2) * 8 + g) * 2 + l))
    return pairs


def _dot(a, b):
    return jnp.dot(a, b, precision=PREC, preferred_element_type=jnp.float32)


def _cross(a, b):
    return lax.dot_general(a, b, (((0,), (0,)), ((), ())), precision=PREC, preferred_element_type=jnp.float32)


def _beside(index, mine, theirs):
    return jnp.where(
        index == 0, jnp.concatenate([mine, theirs], axis=1), jnp.concatenate([theirs, mine], axis=1)
    )


def local(direct, adjoint, cell_weight, right_vecs, left_vecs, inv_root):
    c, h, q = lax.axis_index("c"), lax.axis_index("h"), lax.axis_index("q")
    cells, cols = direct.shape
    modes = right_vecs.shape[1]

    next_direct = lax.ppermute(direct, "q", SWAP)
    next_own = lax.ppermute(adjoint, ("c", "g"), _ring_pairs(False))
    other = lax.ppermute(adjoint, "c", SWAP)
    scale = inv_root[None, :]
    terms = jnp.concatenate([_dot(direct, right_vecs * scale), _dot(adjoint, left_vecs * scale)], axis=1)
    terms = terms.reshape(2, 16, cells // 32, 2 * modes).transpose(1, 0, 2, 3).reshape(cells, 2 * modes)
    terms, other = lax.optimization_barrier((terms, other))
    part = lax.psum_scatter(terms, ("g", "q"), scatter_dimension=0, tiled=True)
    part = part.reshape(2, cells // 32, 2 * modes)

    next_other = lax.ppermute(other, ("c", "g"), _ring_pairs(False))
    own = jnp.where(c == 0, adjoint, next_own)
    other = jnp.where(c == 0, other, next_other)

    pair = _beside(q, direct, next_direct) * cell_weight[:, None]
    both = _beside(h, pair, lax.ppermute(pair, "h", SWAP))
    other_both = lax.ppermute(both, "c", SWAP)

    pieces = []
    for step in range(4):
        product = _cross(own, both) + _cross(other, other_both)
        piece = jnp.stack([product[:, k * cols : (k + 1) * cols] for k in range(4)])
        if step < 3:
            own = lax.ppermute(own, ("c", "g"), _ring_pairs(True))
            other = lax.ppermute(other, ("c", "g"), _ring_pairs(True))
        pieces.append(lax.optimization_barrier(piece))
        if step == 2:
            early = lax.all_to_all(jnp.concatenate(pieces[:2]), ("x", "l"), 0, 0, tiled=True).sum(0)
            own, other, pieces, early = lax.optimization_barrier((own, other, pieces, early))

    late = lax.all_to_all(jnp.concatenate(pieces[2:]), ("x", "l"), 0, 0, tiled=True).sum(0)
    home0 = lax.ppermute(jnp.where(q == 0, early, late), AXES, _home_pairs(0))
    home1 = lax.ppermute(jnp.where(q == 0, late, early), AXES, _home_pairs(1))

    low = (lax.axis_index("x") % 2) * 4 + lax.axis_index("l") * 2 + c
    behind = (lax.axis_index("g") - low) % 8
    arrival = jnp.where(behind < 4, behind, 7 - behind)
    gram = jnp.where(arrival < 2, jnp.concatenate([home0, home1]), jnp.concatenate([home1, home0]))

    keep = lax.dynamic_index_in_dim(part, h, 0, keepdims=False)
    away = lax.dynamic_index_in_dim(part, 1 - h, 0, keepdims=False)
    summed = keep + lax.ppermute(away, "h", SWAP)
    return (gram, summed[:, :modes], summed[:, modes:])


def solution(mesh):
    fine = Mesh(mesh.devices.reshape(SIZES), AXES)
    state, snap = ("x", "l", "c"), ("h", "g", "q")
    in_specs = (P(state, snap), P(state, snap), P(state), P(snap, None), P(snap, None), P())
    out_specs = (P(state, snap), P(state + snap, None), P(state + snap, None))


    return jax.shard_map(local, mesh=fine, in_specs=in_specs, out_specs=out_specs, check_vma=False)
```
